32 devices in a mesh: snap: 2 (over x), band: 8 (over z, y), plane: 2 (over core).
Axes of the slice: x: 2, y: 2, z: 4, core: 2. Of those that a mesh axis runs over, the one named last changes fastest.
Arguments:
- velocity: bfloat16 [72, 2048, 4096], P(('snap', 'plane'), 'band'), parts along dimension 0, may hold values from -6 to 6
- wave_x: int32 [128], replicated, may hold values from 0 to 2047
- wave_z: int32 [128], replicated, may hold values from -1024 to 1023
Outputs:
- spectra: float32 [128, 72, 36, 256], P('band', ('snap', 'plane')), parts along dimension 1
The draws below stay inside these ranges and needn't reach their ends.
There are 2 independent parts, one for each index of `snap`. The reference program is written for one: setup_inputs(seed, part) draws one part's arguments, and reference() takes and returns one part's arrays. A program takes and returns all parts, laid end to end along the dimension named above; an argument that names none is the same for every part. Nothing has to cross between parts.
All inputs are finite; a program needn't handle non-finite values.
Results may differ from the reference program's by a relative error of at most 0.0077.
Values may be sent and summed in bfloat16 or wider, within the bound.
No kernel may reach another device: no remote copies, remote signals or barrier semaphores. Data moves between devices by JAX's collectives and lax.ppermute only.
A program may use at most 128 MiB of HBM per device.

```python
import math
import jax
import jax.numpy as jnp
from jax import lax

NX = 4096
NZ = 2048
KX = 128
KZ = 128
PLANES = 36


def set_ends(values, rng, least, largest):
    extent = values.shape
    spot = [jax.random.randint(jax.random.fold_in(rng, axis), (), 0, extent[axis]) for axis in range(len(extent))]
    values = values.at[tuple(spot)].set(least)
    longest = extent.index(max(extent))
    spot[longest] = (spot[longest] + 1) % extent[longest]
    return values.at[tuple(spot)].set(largest)


def level_of(rng, dims, shards, smallest, largest):
    def one(position, shards_of):
        draws = jax.random.uniform(jax.random.fold_in(jax.random.fold_in(rng, 6), position), (shards_of,), jnp.float32, smallest / len(shards), largest / len(shards))
        return jnp.repeat(jnp.exp(draws), dims[position] // shards_of).reshape((-1,) + (1,) * (len(dims) - position - 1))

    gain = one(*shards[0])
    for cut in shards[1:]:
        gain = gain * one(*cut)
    return gain


def noise(rng, dims, scale, limit, pieces=(), kind=jnp.bfloat16):
    entries = scale * jax.random.normal(rng, dims, jnp.float32)
    if pieces:
        entries = entries * level_of(rng, dims, pieces, -0.22, 0.18)
    return jnp.clip(entries, -limit, limit).astype(kind)


def setup_inputs(seed: int = 0, part: int = 0) -> dict:
    key_list = jax.random.split(jax.random.key(seed), 4)
    part_keys = jax.random.split(jax.random.fold_in(key_list[3], part), 4)
    return {
        "velocity": noise(part_keys[0], (PLANES, NZ, NX), 1.0, 6.0, ((0, 2), (1, 8))),
        "wave_x": set_ends(jax.random.randint(key_list[1], (KX,), 0, NX // 2), jax.random.fold_in(key_list[1], 1), 0, (NX // 2) - 1).astype(jnp.int32),
        "wave_z": set_ends(jax.random.randint(key_list[2], (KZ,), 0 - NZ // 2, NZ // 2), jax.random.fold_in(key_list[2], 1), 0 - NZ // 2, (NZ // 2) - 1).astype(jnp.int32),
    }


full_turn = 2.0 * math.pi

def table_x(wave_x, points):
    positions = jnp.arange(points, dtype=jnp.int32)
    phases = positions[:, None] * wave_x[None, :].astype(jnp.int32) % points
    radians = phases.astype(jnp.float32) * (full_turn / points)
    factor = 1.0 / math.sqrt(points)
    return (jnp.concatenate([jnp.cos(radians), -jnp.sin(radians)], axis=1) * factor).astype(jnp.bfloat16)

def table_z(wave_z, offset, amount, points):
    positions = offset + jnp.arange(amount, dtype=jnp.int32)
    phases = positions[:, None] * wave_z[None, :].astype(jnp.int32) % points
    radians = phases.astype(jnp.float32) * (full_turn / points)
    factor = 1.0 / math.sqrt(points)
    cosine = jnp.cos(radians) * factor
    sine = jnp.sin(radians) * factor
    first = jnp.concatenate([cosine, -sine], axis=1)
    second = jnp.concatenate([sine, cosine], axis=1)
    return jnp.stack([first, second], axis=1).astype(jnp.bfloat16)

def cross_pairs(local_part, remote):
    here = local_part.astype(jnp.float32)
    there = remote.astype(jnp.float32)
    half = here.shape[-1] // 2
    real_here = here[..., :half][:, :, None, :]
    imag_here = here[..., half:][:, :, None, :]
    real_there = there[..., :half][:, None, :, :]
    imag_there = there[..., half:][:, None, :, :]
    real_part = real_here * real_there + imag_here * imag_there
    imag_part = imag_here * real_there - real_here * imag_there
    return jnp.concatenate([real_part, imag_part], axis=-1)

def reference(velocity, wave_x, wave_z):
    planes, rows, points = velocity.shape
    basis = table_x(wave_x, points)
    spectrum = lax.map(lambda layer_rows: jnp.dot(layer_rows, basis, preferred_element_type=jnp.float32).astype(jnp.bfloat16), velocity)
    spectrum = spectrum.reshape(planes, rows, 2, -1)
    basis_z = table_z(wave_z, 0, rows, rows)
    modes = jnp.einsum('pzck,zcm->kpm', spectrum.astype(jnp.float32), basis_z.astype(jnp.float32), precision=lax.Precision.HIGHEST).astype(jnp.bfloat16)
    return cross_pairs(modes, modes)
```

```python
import math

import jax
import jax.numpy as jnp
from jax import lax
from jax.experimental import pallas as pl
from jax.experimental.pallas import tpu as pltpu
from jax.sharding import PartitionSpec as P

full_turn = 2.0 * math.pi
CHUNKS = (1,)
BLOCK = 1


def cos_sin(phases, points):
    radians = (phases % points).astype(jnp.float32) * (full_turn / points)
    return jnp.cos(radians), jnp.sin(radians)


def table_x(wave, points):
    fine = 1 << (points.bit_length() // 2)
    coarse = points // fine
    cos_a, sin_a = cos_sin(fine * jnp.arange(coarse, dtype=jnp.int32)[:, None] * wave[None, :], points)
    cos_b, sin_b = cos_sin(jnp.arange(fine, dtype=jnp.int32)[:, None] * wave[None, :], points)
    factor = 1.0 / math.sqrt(points)
    cos_b, sin_b = cos_b * factor, sin_b * factor
    cos_a, sin_a, cos_b, sin_b = lax.optimization_barrier((cos_a, sin_a, cos_b, sin_b))
    cosine = cos_a[:, None, :] * cos_b[None] - sin_a[:, None, :] * sin_b[None]
    sine = sin_a[:, None, :] * cos_b[None] + cos_a[:, None, :] * sin_b[None]
    both = jnp.concatenate([cosine, -sine], axis=-1)
    return both.astype(jnp.bfloat16).reshape(points, 2 * wave.shape[0])


def table_z(wave, offset, amount, points):
    positions = offset + jnp.arange(amount, dtype=jnp.int32)
    cosine, sine = cos_sin(positions[:, None] * wave[None, :], points)
    factor = 1.0 / math.sqrt(points)
    cosine, sine = cosine * factor, sine * factor
    first = jnp.concatenate([cosine, -sine], axis=1)
    second = jnp.concatenate([sine, cosine], axis=1)
    return jnp.concatenate([first, second], axis=0).astype(jnp.bfloat16)


def transform_body(vel_ref, bx_ref, bz_ref, keep_ref, send_ref):
    block, rows, points = vel_ref.shape
    half, _, own, width = keep_ref.shape
    spec = jnp.dot(
        vel_ref[...].reshape(block * rows, points), bx_ref[...], preferred_element_type=jnp.float32
    ).astype(jnp.bfloat16)
    modes_x = bx_ref.shape[1] // 2
    for p in range(block):
        one = spec[p * rows : (p + 1) * rows]
        both = jnp.concatenate([one[:, :modes_x], one[:, modes_x:]], axis=0)
        modes = lax.dot_general(
            both, bz_ref[...], (((0,), (0,)), ((), ())), preferred_element_type=jnp.float32
        )
        modes = modes.reshape(2, half, own, width)
        keep_ref[:, p] = modes[0]
        send_ref[:, p] = modes[1].astype(jnp.bfloat16)


def transform(velocity, bx, bz, start, count, groups, block):
    _, rows, points = velocity.shape
    own = bx.shape[1] // 2 // groups
    width = bz.shape[1]
    half = groups // 2
    out_block = pl.BlockSpec((half, block, own, width), lambda i: (0, i, 0, 0))
    whole = lambda a: pl.BlockSpec(a.shape, lambda i: (0, 0), pipeline_mode=pl.Buffered(1))
    return pl.pallas_call(
        transform_body,
        out_shape=[
            jax.ShapeDtypeStruct((half, count, own, width), jnp.float32),
            jax.ShapeDtypeStruct((half, count, own, width), jnp.bfloat16),
        ],
        grid=(count // block,),
        in_specs=[
            pl.BlockSpec((block, rows, points), lambda i: (start // block + i, 0, 0)),
            whole(bx),
            whole(bz),
        ],
        out_specs=[out_block, out_block],
        cost_estimate=pl.CostEstimate(
            flops=2 * count * rows * points * bx.shape[1],
            bytes_accessed=2 * count * rows * points,
            transcendentals=0,
        ),
        name="transform",
    )(velocity, bx, bz)


def pairs_body(side_ref, here_ref, own_ref, other_ref, out_ref):
    step, there, _, width = out_ref.shape
    planes = there // 2
    half = width // 2
    side = side_ref[0]
    here = here_ref[...].astype(jnp.float32)
    for g, ref in enumerate((own_ref, other_ref)):
        offset = planes * (side if g == 0 else 1 - side)
        for i in range(step):
            real_i, imag_i = here[i, :, :half], here[i, :, half:]
            for j in range(planes):
                pair = ref[j].astype(jnp.float32)
                real_j, imag_j = pair[:, :half], pair[:, half:]
                out_ref[i, offset + j, :, :half] = real_i * real_j + imag_i * imag_j
                out_ref[i, offset + j, :, half:] = imag_i * real_j - real_i * imag_j


def pairs(mine, other, side, step):
    planes, own, width = mine.shape
    full = pl.BlockSpec(mine.shape, lambda i, s: (0, 0, 0))
    return pl.pallas_call(
        pairs_body,
        out_shape=jax.ShapeDtypeStruct((planes, 2 * planes, own, width), jnp.float32),
        grid_spec=pltpu.PrefetchScalarGridSpec(
            num_scalar_prefetch=1,
            grid=(planes // step,),
            in_specs=[pl.BlockSpec((step, own, width), lambda i, s: (i, 0, 0)), full, full],
            out_specs=pl.BlockSpec((step, 2 * planes, own, width), lambda i, s: (i, 0, 0, 0)),
        ),
        name="pairs",
    )(side, mine, mine, other)


def partner(groups, bits):
    return [(i, i ^ bits) for i in range(groups)]


def shards(velocity, wave_x, wave_z):
    planes, rows, points = velocity.shape
    groups = lax.axis_size("band")
    me = lax.axis_index("band")
    side = lax.axis_index("plane")
    modes_x = wave_x.shape[0]
    own = modes_x // groups
    wave = wave_x.reshape(groups, own)
    bit = 1
    while bit < groups:
        swapped = jnp.flip(wave.reshape(-1, 2, bit, own), axis=1).reshape(groups, own)
        wave = jnp.where((me & bit) != 0, swapped, wave)
        bit *= 2
    wave = wave.reshape(groups // 2, 2, own).transpose(1, 0, 2).reshape(modes_x)
    bx = table_x(wave, points)
    bz = table_z(wave_z, me * rows, rows, rows * groups)

    total = sum(CHUNKS)
    sizes = [planes * c // total for c in CHUNKS]
    start = 0
    mine = []
    for size in sizes:
        keep, send = transform(velocity, bx, bz, start, size, groups, BLOCK)
        start += size
        got = lax.ppermute(send, "band", partner(groups, 1))
        summed = keep + got.astype(jnp.float32)
        acc = summed[0]
        for d in range(1, groups // 2):
            acc = acc + lax.ppermute(
                summed[d].astype(jnp.bfloat16), "band", partner(groups, 2 * d)
            ).astype(jnp.float32)
        mine.append(acc.astype(jnp.bfloat16))
    mine = jnp.concatenate(mine, axis=0)
    other = lax.ppermute(mine, "plane", [(0, 1), (1, 0)])
    out = pairs(mine, other, side[None], 2)
    return out.transpose(2, 0, 1, 3)


def solution(mesh):
    in_specs = (P(("snap", "plane"), "band", None), P(), P())
    out_specs = P("band", ("snap", "plane"), None, None)
    return jax.shard_map(shards, mesh=mesh, in_specs=in_specs, out_specs=out_specs, check_vma=False)
```

```python
import functools
import math

import jax
import jax.numpy as jnp
from jax import lax
from jax.experimental import pallas as pl
from jax.experimental.pallas import tpu as pltpu
from jax.sharding import PartitionSpec as P

full_turn = 2.0 * math.pi
CHUNKS = (9, 9)


def split(points):
    fine = 1 << (points.bit_length() // 2)
    return fine, points // fine


def angles(wave_x, points_x, wave_z, offset, rows, points_z):
    fine_x, coarse_x = split(points_x)
    fine_z, coarse_z = split(rows)
    first = fine_x + coarse_x
    row = lax.broadcasted_iota(jnp.int32, (first + fine_z + coarse_z, wave_x.shape[0]), 0)
    place_x = jnp.where(row < fine_x, row, (row - fine_x) * fine_x)
    row_z = row - first
    place_z = jnp.where(row_z < fine_z, row_z, offset + (row_z - fine_z) * fine_z)
    in_x = row < first
    phase = jnp.where(
        in_x, place_x * wave_x[None, :] & (points_x - 1), place_z * wave_z[None, :] & (points_z - 1)
    )
    radians = phase.astype(jnp.float32) * jnp.where(in_x, full_turn / points_x, full_turn / points_z)
    return jnp.cos(radians), jnp.sin(radians)


def fill_tables(cos_ref, sin_ref, bx_ref, bz_ref, points_z):
    points_x, modes = bx_ref.shape[0], bx_ref.shape[1] // 2
    rows = bz_ref.shape[0] // 2
    fine, coarse = split(points_x)
    factor = 1.0 / math.sqrt(points_x)
    cos_b, sin_b = cos_ref[:fine] * factor, sin_ref[:fine] * factor

    def fill_x(a, carry):
        cos_a, sin_a = cos_ref[pl.ds(fine + a, 1)], sin_ref[pl.ds(fine + a, 1)]
        at = pl.ds(pl.multiple_of(a * fine, fine), fine)
        bx_ref[at, :modes] = (cos_a * cos_b - sin_a * sin_b).astype(jnp.bfloat16)
        bx_ref[at, modes:] = -(sin_a * cos_b + cos_a * sin_b).astype(jnp.bfloat16)
        return carry

    lax.fori_loop(0, coarse, fill_x, 0)
    first = fine + coarse
    fine, coarse = split(rows)
    factor = 1.0 / math.sqrt(points_z)
    cos_d, sin_d = cos_ref[first : first + fine] * factor, sin_ref[first : first + fine] * factor

    def fill_z(a, carry):
        at = first + fine + a
        cos_c, sin_c = cos_ref[pl.ds(at, 1)], sin_ref[pl.ds(at, 1)]
        cosine = (cos_c * cos_d - sin_c * sin_d).astype(jnp.bfloat16)
        sine = (sin_c * cos_d + cos_c * sin_d).astype(jnp.bfloat16)
        top = pl.ds(pl.multiple_of(a * fine, fine), fine)
        low = pl.ds(pl.multiple_of(rows + a * fine, fine), fine)
        bz_ref[top, :modes] = cosine
        bz_ref[top, modes:] = -sine
        bz_ref[low, :modes] = sine
        bz_ref[low, modes:] = cosine
        return carry

    lax.fori_loop(0, coarse, fill_z, 0)


def transform_body(start, first, points_z, vel_ref, one_ref, two_ref, *rest):
    if first:
        keep_ref, send_ref, bx_ref, bz_ref, buf, spec, sem = rest
    else:
        bx_ref, bz_ref = one_ref, two_ref
        keep_ref, send_ref, buf, spec, sem = rest
    half, count, own, width = keep_ref.shape
    modes_x = bx_ref.shape[1] // 2

    def fetch(p):
        return pltpu.make_async_copy(vel_ref.at[start + p], buf.at[p], sem.at[p])

    for p in range(count):
        fetch(p).start()
    if first:
        fill_tables(one_ref, two_ref, bx_ref, bz_ref, points_z)

    def along_x(p):
        fetch(p).wait()
        out = jnp.dot(buf[p], bx_ref[...], preferred_element_type=jnp.float32)
        spec[p % 2] = out.astype(jnp.bfloat16)

    def along_z(p):
        one = spec[p % 2]
        both = jnp.concatenate([one[:, :modes_x], one[:, modes_x:]], axis=0)
        modes = lax.dot_general(
            both, bz_ref[...], (((0,), (0,)), ((), ())), preferred_element_type=jnp.float32
        ).reshape(2, half, own, width)
        keep_ref[:, p] = modes[0]
        send_ref[:, p] = modes[1].astype(jnp.bfloat16)

    along_x(0)

    def step(p, carry):
        along_z(p - 1)
        along_x(p)
        return carry

    lax.fori_loop(1, count, step, 0)
    along_z(count - 1)


def transform(velocity, one, two, start, count, first, groups, points_z, modes_x, modes_z):
    _, rows, points = velocity.shape
    own, half = modes_x // groups, groups // 2
    width = 2 * modes_z
    vmem = pl.BlockSpec(memory_space=pltpu.VMEM)
    outs = [
        jax.ShapeDtypeStruct((half, count, own, width), jnp.float32),
        jax.ShapeDtypeStruct((half, count, own, width), jnp.bfloat16),
    ]
    if first:
        outs += [
            jax.ShapeDtypeStruct((points, 2 * modes_x), jnp.bfloat16),
            jax.ShapeDtypeStruct((2 * rows, width), jnp.bfloat16),
        ]
    scratch = 2 * count * rows * points
    return pl.pallas_call(
        functools.partial(transform_body, start, first, points_z),
        out_shape=outs,
        in_specs=[pl.BlockSpec(memory_space=pl.ANY), vmem, vmem],
        out_specs=[vmem] * len(outs),
        scratch_shapes=[
            pltpu.VMEM((count, rows, points), velocity.dtype),
            pltpu.VMEM((2, rows, 2 * modes_x), jnp.bfloat16),
            pltpu.SemaphoreType.DMA((count,)),
        ],
        compiler_params=pltpu.CompilerParams(vmem_limit_bytes=scratch + (8 << 20)),
        cost_estimate=pl.CostEstimate(
            flops=4 * count * rows * points * modes_x,
            bytes_accessed=scratch,
            transcendentals=0,
        ),
        name=f"transform{start}",
    )(velocity, one, two)


def pairs_body(side_ref, here_ref, own_ref, other_ref, out_ref):
    step, there, _, width = out_ref.shape
    planes = there // 2
    half = width // 2
    side = side_ref[0]
    here = here_ref[...].astype(jnp.float32)
    for g, ref in enumerate((own_ref, other_ref)):
        offset = planes * (side if g == 0 else 1 - side)
        for i in range(step):
            real_i, imag_i = here[i, :, :half], here[i, :, half:]
            for j in range(planes):
                pair = ref[j].astype(jnp.float32)
                real_j, imag_j = pair[:, :half], pair[:, half:]
                out_ref[i, offset + j, :, :half] = real_i * real_j + imag_i * imag_j
                out_ref[i, offset + j, :, half:] = imag_i * real_j - real_i * imag_j


def pairs(mine, other, side, step):
    planes, own, width = mine.shape
    full = pl.BlockSpec(mine.shape, lambda i, s: (0, 0, 0))
    return pl.pallas_call(
        pairs_body,
        out_shape=jax.ShapeDtypeStruct((planes, 2 * planes, own, width), jnp.float32),
        grid_spec=pltpu.PrefetchScalarGridSpec(
            num_scalar_prefetch=1,
            grid=(planes // step,),
            in_specs=[pl.BlockSpec((step, own, width), lambda i, s: (i, 0, 0)), full, full],
            out_specs=pl.BlockSpec((step, 2 * planes, own, width), lambda i, s: (i, 0, 0, 0)),
        ),
        name="pairs",
    )(side, mine, mine, other)


def partner(groups, bits):
    return [(i, i ^ bits) for i in range(groups)]


def partner(groups, bits):
    return [(i, i ^ bits) for i in range(groups)]


def shards(velocity, wave_x, wave_z):
    planes, rows, points = velocity.shape
    groups = lax.axis_size("band")
    me = lax.axis_index("band")
    side = lax.axis_index("plane")
    modes_x, modes_z = wave_x.shape[0], wave_z.shape[0]
    own = modes_x // groups
    wave = wave_x.reshape(groups, own)
    bit = 1
    while bit < groups:
        swapped = jnp.flip(wave.reshape(-1, 2, bit, own), axis=1).reshape(groups, own)
        wave = jnp.where((me & bit) != 0, swapped, wave)
        bit *= 2
    wave = wave.reshape(groups // 2, 2, own).transpose(1, 0, 2).reshape(modes_x)
    cosine, sine = angles(wave, points, wave_z, me * rows, rows, rows * groups)

    total = sum(CHUNKS)
    ends = [0]
    for c in CHUNKS:
        ends.append(ends[-1] + c)
    ends = [planes * e // total for e in ends]
    tables = (cosine, sine)
    mine, others = [], []
    for start, stop in zip(ends[:-1], ends[1:]):
        got = transform(
            velocity, *tables, start, stop - start, start == 0, groups, rows * groups, modes_x, modes_z
        )
        keep, send = got[:2]
        if start == 0:
            tables = got[2:]
        got = lax.ppermute(send, "band", partner(groups, 1))
        summed = keep + got.astype(jnp.float32)
        acc = summed[0]
        for d in range(1, groups // 2):
            acc = acc + lax.ppermute(
                summed[d].astype(jnp.bfloat16), "band", partner(groups, 2 * d)
            ).astype(jnp.float32)
        acc = acc.astype(jnp.bfloat16)
        mine.append(acc)
        others.append(lax.ppermute(acc, "plane", [(0, 1), (1, 0)]))
    out = pairs(jnp.concatenate(mine, axis=0), jnp.concatenate(others, axis=0), side[None], 2)
    return out.transpose(2, 0, 1, 3)


def solution(mesh):
    in_specs = (P(("snap", "plane"), "band", None), P(), P())
    out_specs = P("band", ("snap", "plane"), None, None)
    return jax.shard_map(shards, mesh=mesh, in_specs=in_specs, out_specs=out_specs, check_vma=False)
```

```python
import functools
import math

import jax
import jax.numpy as jnp
from jax import lax
from jax.experimental import pallas as pl
from jax.experimental.pallas import tpu as pltpu
from jax.sharding import PartitionSpec as P


full_turn = 2.0 * math.pi
CHUNKS = (11,7)


def split(points):
    fine = 1 << (points.bit_length() // 2)
    return fine, points // fine


def cos_sin(phase, points):
    radians = (phase & (points - 1)).astype(jnp.float32) * (full_turn / points)
    return jnp.cos(radians), jnp.sin(radians)


def fill_table(wave, offset, amount, points, store):
    fine, coarse = split(amount)
    lanes = wave.shape[1]
    row = lax.broadcasted_iota(jnp.int32, (fine, lanes), 0)
    cos_b, sin_b = cos_sin(row * wave, points)
    factor = 1.0 / math.sqrt(points)
    cos_b, sin_b = cos_b * factor, sin_b * factor
    batch = 8
    row = lax.broadcasted_iota(jnp.int32, (batch, lanes), 0)

    def fill(g, carry):
        cos_a, sin_a = cos_sin((offset + (row + g * batch) * fine) * wave, points)
        for r in range(batch):
            cos_r, sin_r = cos_a[r : r + 1], sin_a[r : r + 1]
            cosine = (cos_r * cos_b - sin_r * sin_b).astype(jnp.bfloat16)
            sine = (sin_r * cos_b + cos_r * sin_b).astype(jnp.bfloat16)
            store(pl.multiple_of((g * batch + r) * fine, fine), fine, cosine, sine)
        return carry

    lax.fori_loop(0, coarse // batch, fill, 0)


def fill_tables(me, groups, wave_x, wave_z, bx_ref, bz_ref):
    points_x, modes = bx_ref.shape[0], bx_ref.shape[1] // 2
    rows = bz_ref.shape[0] // 2
    own = modes // groups
    wave = jnp.broadcast_to(wave_x, (8, modes))
    lane = lax.broadcasted_iota(jnp.int32, wave.shape, 1)
    bit = 1
    while bit < groups:
        shift = bit * own
        swapped = jnp.where(
            (lane & shift) != 0, pltpu.roll(wave, shift, 1), pltpu.roll(wave, modes - shift, 1)
        )
        wave = jnp.where((me & bit) != 0, swapped, wave)
        bit *= 2

    def store_x(at, size, cosine, sine):
        bx_ref[pl.ds(at, size), :modes] = cosine
        bx_ref[pl.ds(at, size), modes:] = -sine

    def store_z(at, size, cosine, sine):
        bz_ref[pl.ds(at, size), :modes] = cosine
        bz_ref[pl.ds(at, size), modes:] = -sine
        bz_ref[pl.ds(rows + at, size), :modes] = sine
        bz_ref[pl.ds(rows + at, size), modes:] = cosine

    fill_table(wave[:1], 0, points_x, points_x, store_x)
    fill_table(wave_z, me * rows, rows, rows * groups, store_z)


def transform_body(start, first, last, groups, vel_ref, *rest):
    if first:
        wave_x_ref, wave_z_ref, *rest = rest
    else:
        bx_ref, bz_ref, ready_ref, *rest = rest
    keep_ref, send_ref, *rest = rest
    if first:
        bx_ref, bz_ref, *rest = rest
    if not last:
        next_ref, *rest = rest
    buf, spec, sem, *rest = rest
    half, count, own, width = keep_ref.shape
    modes_x = bx_ref.shape[1] // 2
    held = 0 if first else 1

    def fetch(p):
        return pltpu.make_async_copy(vel_ref.at[start + p], buf.at[p - held], sem.at[p])

    if first:
        waves, wave_sem = rest
        wave_copies = [
            pltpu.make_async_copy(ref, waves.at[i], wave_sem.at[i])
            for i, ref in enumerate((wave_x_ref, wave_z_ref))
        ]
        for copy in wave_copies:
            copy.start()
    early = 1 if first else count
    for p in range(held, early):
        fetch(p).start()
    if first:
        for copy in wave_copies:
            copy.wait()
        for p in range(early, count):
            fetch(p).start()
    if not last:
        ahead = pltpu.make_async_copy(vel_ref.at[start + count], next_ref, sem.at[count])
        ahead.start()
    if first:
        fill_tables(lax.axis_index("band"), groups, waves[0], waves[1], bx_ref, bz_ref)

    def along_x(p, plane):
        out = jnp.dot(plane, bx_ref[...], preferred_element_type=jnp.float32)
        spec[p % 2] = out.astype(jnp.bfloat16)

    def along_z(p, one):
        both = jnp.concatenate([one[:, :modes_x], one[:, modes_x:]], axis=0)
        modes = lax.dot_general(
            both, bz_ref[...], (((0,), (0,)), ((), ())), preferred_element_type=jnp.float32
        ).reshape(half, 2, own, width)
        keep_ref[:, p] = modes[:, 0]
        send_ref[:, p] = modes[:, 1].astype(jnp.bfloat16)

    if first:
        fetch(0).wait()
        along_x(0, buf[0])
    else:
        along_x(0, ready_ref[...])

    def step(p, carry):
        fetch(p).wait()
        before = spec[(p - 1) % 2]
        along_x(p, buf[p - held])
        along_z(p - 1, before)
        return carry

    lax.fori_loop(1, count, step, 0)
    along_z(count - 1, spec[(count - 1) % 2])
    if not last:
        ahead.wait()


def transform(velocity, tables, start, count, groups, modes_x, modes_z):
    planes, rows, points = velocity.shape
    first, last = start == 0, start + count == planes
    own, half = modes_x // groups, groups // 2
    width = 2 * modes_z
    vmem = pl.BlockSpec(memory_space=pltpu.VMEM)
    hbm = pl.BlockSpec(memory_space=pltpu.HBM)
    outs = [
        jax.ShapeDtypeStruct((half, count, own, width), jnp.float32),
        jax.ShapeDtypeStruct((half, count, own, width), jnp.bfloat16),
    ]
    more = []
    if first:
        outs += [
            jax.ShapeDtypeStruct((points, 2 * modes_x), jnp.bfloat16),
            jax.ShapeDtypeStruct((2 * rows, width), jnp.bfloat16),
        ]
        more = [pltpu.VMEM((2, *tables[0].shape), jnp.int32), pltpu.SemaphoreType.DMA((2,))]
        tables = [pltpu.with_memory_space_constraint(t, pltpu.HBM) for t in tables]
    if not last:
        outs.append(jax.ShapeDtypeStruct((rows, points), velocity.dtype))
    slots = count if first else count - 1
    scratch = 2 * slots * rows * points
    return pl.pallas_call(
        functools.partial(transform_body, start, first, last, groups),
        out_shape=outs,
        in_specs=[hbm] + [hbm if first else vmem] * len(tables),
        out_specs=[vmem] * len(outs),
        scratch_shapes=[
            pltpu.VMEM((slots, rows, points), velocity.dtype),
            pltpu.VMEM((2, rows, 2 * modes_x), jnp.bfloat16),
            pltpu.SemaphoreType.DMA((count + 1,)),
            *more,
        ],
        compiler_params=pltpu.CompilerParams(vmem_limit_bytes=scratch + (8 << 20)),
        cost_estimate=pl.CostEstimate(
            flops=4 * count * rows * points * modes_x,
            bytes_accessed=scratch,
            transcendentals=0,
        ),
    )(velocity, *tables)


def pairs_body(start, pieces, *refs):
    me = lax.axis_index("plane")
    mine, others = refs[:pieces], refs[pieces : 2 * pieces]
    refs = refs[2 * pieces + (1 if start else 0) :]
    out_ref, both, rows_buf, rows_sem = refs[:4]
    _, stop, _, width = both.shape
    half = width // 2
    planes = out_ref.shape[0]
    for side, group in enumerate((mine, others)):
        at = 0
        for ref in group:
            both[side, at : at + ref.shape[0]] = ref[...].astype(jnp.float32)
            at += ref.shape[0]

    def sweep(first_i, last_i, first_j, buf, sem):
        count = stop - first_j

        def copy(i, g):
            offset = planes * (me if g == 0 else 1 - me)
            return pltpu.make_async_copy(
                buf.at[i - first_i, g],
                out_ref.at[i, pl.ds(offset + first_j, count)],
                sem.at[i - first_i, g],
            )

        def one(i, carry):
            here = both[0, i]
            real_i, imag_i = here[:, :half], here[:, half:]
            for g in range(2):
                for j in range(count):
                    there = both[g, first_j + j]
                    real_j, imag_j = there[:, :half], there[:, half:]
                    buf[i - first_i, g, j, :, :half] = real_i * real_j + imag_i * imag_j
                    buf[i - first_i, g, j, :, half:] = imag_i * real_j - real_i * imag_j
                copy(i, g).start()
            return carry

        lax.fori_loop(first_i, last_i, one, 0)

        def finish():
            def one_wait(i, carry):
                copy(i, 0).wait()
                copy(i, 1).wait()
                return carry

            lax.fori_loop(first_i, last_i, one_wait, 0)

        return finish

    finish = [sweep(start, stop, 0, rows_buf, rows_sem)]
    if start:
        finish.append(sweep(0, start, start, *refs[4:]))
    for wait in finish:
        wait()


def pairs(mine, others, start, planes, before):
    pieces = len(mine)
    _, own, width = mine[0].shape
    count = mine[-1].shape[0]
    stop = start + count
    vmem = pl.BlockSpec(memory_space=pltpu.VMEM)
    hbm = pl.BlockSpec(memory_space=pltpu.HBM)
    scratch = [
        pltpu.VMEM((2, stop, own, width), jnp.float32),
        pltpu.VMEM((count, 2, stop, own, width), jnp.float32),
        pltpu.SemaphoreType.DMA((count, 2)),
    ]
    held = (2 * stop + 2 * count * stop) * own * width * 4
    args = [*mine, *others]
    if start:
        scratch += [
            pltpu.VMEM((start, 2, count, own, width), jnp.float32),
            pltpu.SemaphoreType.DMA((start, 2)),
        ]
        held += 2 * start * count * own * width * 4
        args.append(before)
    return pl.pallas_call(
        functools.partial(pairs_body, start, pieces),
        out_shape=jax.ShapeDtypeStruct((planes, 2 * planes, own, width), jnp.float32),
        in_specs=[vmem] * (2 * pieces) + [hbm] * (1 if start else 0),
        out_specs=hbm,
        scratch_shapes=scratch,
        input_output_aliases={2 * pieces: 0} if start else {},
        compiler_params=pltpu.CompilerParams(vmem_limit_bytes=held + (6 << 20)),
        cost_estimate=pl.CostEstimate(
            flops=6 * held // 4, bytes_accessed=held, transcendentals=0
        ),
    )(*args)


def partner(groups, bits):
    return [(i, i ^ bits) for i in range(groups)]


def exchange(keep, send, groups):
    bit = 1
    while True:
        got = lax.ppermute(send, "band", partner(groups, bit))
        if 2 * bit == groups:
            return (keep[0] + got[0].astype(jnp.float32)).astype(jnp.bfloat16)
        halves = (-1, 2, *keep.shape[1:])
        keep, got = keep.reshape(halves), got.reshape(halves)
        send = (keep[:, 1] + got[:, 1].astype(jnp.float32)).astype(jnp.bfloat16)
        keep, got, send = lax.optimization_barrier((keep, got, send))
        keep = lax.optimization_barrier(keep[:, 0] + got[:, 0].astype(jnp.float32))
        bit *= 2


def shards(velocity, wave_x, wave_z):
    planes, _, _ = velocity.shape
    groups = lax.axis_size("band")
    modes_x, modes_z = wave_x.shape[0], wave_z.shape[0]
    total = sum(CHUNKS)
    ends = [0]
    for c in CHUNKS:
        ends.append(ends[-1] + c)
    ends = [planes * e // total for e in ends]
    tables = [wave_x[None], wave_z[None]]
    mine, others, out = [], [], None
    for start, stop in zip(ends[:-1], ends[1:]):
        got = transform(velocity, tables, start, stop - start, groups, modes_x, modes_z)
        tables = [*got[2:4], *got[4:]] if start == 0 else [*tables[:2], *got[2:]]
        piece = exchange(*got[:2], groups)
        mine.append(piece)
        others.append(lax.ppermute(piece, "plane", [(0, 1), (1, 0)]))
        out = pairs(mine, others, start, planes, out)
    return out.transpose(2, 0, 1, 3)


def solution(mesh):
    in_specs = (P(("snap", "plane"), "band", None), P(), P())
    out_specs = P("band", ("snap", "plane"), None, None)
    return jax.shard_map(shards, mesh=mesh, in_specs=in_specs, out_specs=out_specs, check_vma=False)
```

```python
import functools
import math

import jax
import jax.numpy as jnp
from jax import lax
from jax.experimental import pallas as pl
from jax.experimental.pallas import tpu as pltpu
from jax.sharding import PartitionSpec as P


full_turn = 2.0 * math.pi
CHUNKS = (10, 8)
BLOCKS = (2, 1)


def split(points):
    fine = 1 << (points.bit_length() // 2)
    return fine, points // fine


def cos_sin(phase, points):
    radians = (phase & (points - 1)).astype(jnp.float32) * (full_turn / points)
    return jnp.cos(radians), jnp.sin(radians)


def fill_table(wave, offset, amount, points, store):
    fine, coarse = split(amount)
    lanes = wave.shape[1]
    row = lax.broadcasted_iota(jnp.int32, (fine, lanes), 0)
    cos_b, sin_b = cos_sin(row * wave, points)
    factor = 1.0 / math.sqrt(points)
    cos_b, sin_b = cos_b * factor, sin_b * factor
    batch = 8
    row = lax.broadcasted_iota(jnp.int32, (batch, lanes), 0)

    def fill(g, carry):
        cos_a, sin_a = cos_sin((offset + (row + g * batch) * fine) * wave, points)
        for r in range(batch):
            cos_r, sin_r = cos_a[r : r + 1], sin_a[r : r + 1]
            cosine = (cos_r * cos_b - sin_r * sin_b).astype(jnp.bfloat16)
            sine = (sin_r * cos_b + cos_r * sin_b).astype(jnp.bfloat16)
            store(pl.multiple_of((g * batch + r) * fine, fine), fine, cosine, sine)
        return carry

    lax.fori_loop(0, coarse // batch, fill, 0)


def fill_tables(me, groups, wave_x, wave_z, bx_ref, bz_ref):
    points_x, modes = bx_ref.shape[0], bx_ref.shape[1] // 2
    rows = bz_ref.shape[0] // 2
    own = modes // groups
    wave = jnp.broadcast_to(wave_x, (8, modes))
    lane = lax.broadcasted_iota(jnp.int32, wave.shape, 1)
    bit = 1
    while bit < groups:
        shift = bit * own
        swapped = jnp.where(
            (lane & shift) != 0, pltpu.roll(wave, shift, 1), pltpu.roll(wave, modes - shift, 1)
        )
        wave = jnp.where((me & bit) != 0, swapped, wave)
        bit *= 2

    def store_x(at, size, cosine, sine):
        bx_ref[pl.ds(at, size), :modes] = cosine
        bx_ref[pl.ds(at, size), modes:] = -sine

    def store_z(at, size, cosine, sine):
        bz_ref[pl.ds(at, size), :modes] = cosine
        bz_ref[pl.ds(at, size), modes:] = -sine
        bz_ref[pl.ds(rows + at, size), :modes] = sine
        bz_ref[pl.ds(rows + at, size), modes:] = cosine

    fill_table(wave[:1], 0, points_x, points_x, store_x)
    fill_table(wave_z, me * rows, rows, rows * groups, store_z)


def transform_body(start, count, first, last, groups, vel_ref, *rest):
    if first:
        wave_x_ref, wave_z_ref, *rest = rest
    else:
        bx_ref, bz_ref, ready_ref, *rest = rest
    keep_ref, send_ref, *rest = rest
    if first:
        bx_ref, bz_ref, *rest = rest
    if not last:
        next_ref, *rest = rest
    buf, spec, sem, *rest = rest
    paths, half, path_count, own, width = keep_ref.shape
    modes_x = bx_ref.shape[1] // 2
    block = spec.shape[1] // vel_ref.shape[1]
    held = 0 if first else block

    def fetch(p):
        return pltpu.make_async_copy(vel_ref.at[start + p], buf.at[p - held], sem.at[p])

    if first:
        waves, wave_sem = rest
        wave_copies = [
            pltpu.make_async_copy(ref, waves.at[i], wave_sem.at[i])
            for i, ref in enumerate((wave_x_ref, wave_z_ref))
        ]
        for copy in wave_copies:
            copy.start()
    early = 1 if first else count
    for p in range(held, early):
        fetch(p).start()
    if first:
        for copy in wave_copies:
            copy.wait()
        for p in range(early, count):
            fetch(p).start()
    if not last:
        ahead = pltpu.make_async_copy(
            vel_ref.at[pl.ds(start + count, next_ref.shape[0])], next_ref, sem.at[count]
        )
        ahead.start()
    if first:
        fill_tables(lax.axis_index("band"), groups, waves[0], waves[1], bx_ref, bz_ref)

    rows, points = vel_ref.shape[1:]

    def along_x(g, planes):
        out = jnp.dot(
            planes.reshape(block * rows, points), bx_ref[...], preferred_element_type=jnp.float32
        )
        spec[g % 2] = out.astype(jnp.bfloat16)

    def along_z(g, many):
        for k in range(block):
            one = many[k * rows : (k + 1) * rows]
            both = jnp.concatenate([one[:, :modes_x], one[:, modes_x:]], axis=0)
            modes = lax.dot_general(
                both, bz_ref[...], (((0,), (0,)), ((), ())), preferred_element_type=jnp.float32
            ).reshape(half // 2, 2, 2, own, width)
            p = g * block + k
            path = 0
            below, above = modes[:, 1, 0], modes[:, 0, 1]
            if paths == 2:
                path = jnp.asarray(p >= path_count).astype(jnp.int32)
                below, above = jnp.where(path == 1, above, below), jnp.where(path == 1, below, above)
            p = p - path * path_count
            for part in range(half // 2):
                keep_ref[path, 2 * part, p] = modes[part, 0, 0]
                keep_ref[path, 2 * part + 1, p] = below[part]
                send_ref[path, 2 * part, p] = above[part].astype(jnp.bfloat16)
                send_ref[path, 2 * part + 1, p] = modes[part, 1, 1].astype(jnp.bfloat16)

    def arrive(g):
        for k in range(block):
            fetch(g * block + k).wait()

    if first:
        arrive(0)
        along_x(0, buf[:block])
    else:
        along_x(0, ready_ref[...])

    def step(g, carry):
        arrive(g)
        before = spec[(g - 1) % 2]
        along_x(g, buf[pl.ds(g * block - held, block)])
        along_z(g - 1, before)
        return carry

    steps = count // block
    lax.fori_loop(1, steps, step, 0)
    along_z(steps - 1, spec[(steps - 1) % 2])
    if not last:
        ahead.wait()


def transform(velocity, tables, start, count, block, ahead, paths, groups, modes_x, modes_z):
    planes, rows, points = velocity.shape
    first, last = start == 0, start + count == planes
    own, half = modes_x // groups, groups // 2
    width = 2 * modes_z
    vmem = pl.BlockSpec(memory_space=pltpu.VMEM)
    hbm = pl.BlockSpec(memory_space=pltpu.HBM)
    outs = [
        jax.ShapeDtypeStruct((paths, half, -(-count // paths), own, width), jnp.float32),
        jax.ShapeDtypeStruct((paths, half, -(-count // paths), own, width), jnp.bfloat16),
    ]
    more = []
    if first:
        outs += [
            jax.ShapeDtypeStruct((points, 2 * modes_x), jnp.bfloat16),
            jax.ShapeDtypeStruct((2 * rows, width), jnp.bfloat16),
        ]
        more = [pltpu.VMEM((2, *tables[0].shape), jnp.int32), pltpu.SemaphoreType.DMA((2,))]
        tables = [pltpu.with_memory_space_constraint(t, pltpu.HBM) for t in tables]
    if not last:
        outs.append(jax.ShapeDtypeStruct((ahead, rows, points), velocity.dtype))
    slots = count if first else count - block
    scratch = 2 * slots * rows * points
    return pl.pallas_call(
        functools.partial(transform_body, start, count, first, last, groups),
        out_shape=outs,
        in_specs=[hbm] + [hbm if first else vmem] * len(tables),
        out_specs=[vmem] * len(outs),
        scratch_shapes=[
            pltpu.VMEM((slots, rows, points), velocity.dtype),
            pltpu.VMEM((2, block * rows, 2 * modes_x), jnp.bfloat16),
            pltpu.SemaphoreType.DMA((count + 1,)),
            *more,
        ],
        compiler_params=pltpu.CompilerParams(vmem_limit_bytes=scratch + (8 << 20)),
        cost_estimate=pl.CostEstimate(
            flops=4 * count * rows * points * modes_x,
            bytes_accessed=scratch,
            transcendentals=0,
        ),
    )(velocity, *tables)


def pairs_body(start, pieces, *refs):
    me = lax.axis_index("plane")
    mine, others = refs[:pieces], refs[pieces : 2 * pieces]
    refs = refs[2 * pieces + (1 if start else 0) :]
    out_ref, both, rows_buf, rows_sem = refs[:4]
    _, stop, _, width = both.shape
    half = width // 2
    planes = out_ref.shape[0]
    for side, group in enumerate((mine, others)):
        at = 0
        for ref in group:
            both[side, at : at + ref.shape[0]] = ref[...].astype(jnp.float32)
            at += ref.shape[0]

    def sweep(first_i, last_i, first_j, buf, sem):
        count = stop - first_j

        def copy(i, g):
            offset = planes * (me if g == 0 else 1 - me)
            return pltpu.make_async_copy(
                buf.at[i - first_i, g],
                out_ref.at[i, pl.ds(offset + first_j, count)],
                sem.at[i - first_i, g],
            )

        def one(i, carry):
            here = both[0, i]
            real_i, imag_i = here[:, :half], here[:, half:]
            for g in range(2):
                for j in range(count):
                    there = both[g, first_j + j]
                    real_j, imag_j = there[:, :half], there[:, half:]
                    buf[i - first_i, g, j, :, :half] = real_i * real_j + imag_i * imag_j
                    buf[i - first_i, g, j, :, half:] = imag_i * real_j - real_i * imag_j
                copy(i, g).start()
            return carry

        lax.fori_loop(first_i, last_i, one, 0)

        def finish():
            def one_wait(i, carry):
                copy(i, 0).wait()
                copy(i, 1).wait()
                return carry

            lax.fori_loop(first_i, last_i, one_wait, 0)

        return finish

    finish = [sweep(start, stop, 0, rows_buf, rows_sem)]
    if start:
        finish.append(sweep(0, start, start, *refs[4:]))
    for wait in finish:
        wait()


def pairs(mine, others, start, planes, before):
    pieces = len(mine)
    _, own, width = mine[0].shape
    count = mine[-1].shape[0]
    stop = start + count
    vmem = pl.BlockSpec(memory_space=pltpu.VMEM)
    hbm = pl.BlockSpec(memory_space=pltpu.HBM)
    scratch = [
        pltpu.VMEM((2, stop, own, width), jnp.float32),
        pltpu.VMEM((count, 2, stop, own, width), jnp.float32),
        pltpu.SemaphoreType.DMA((count, 2)),
    ]
    held = (2 * stop + 2 * count * stop) * own * width * 4
    args = [*mine, *others]
    if start:
        scratch += [
            pltpu.VMEM((start, 2, count, own, width), jnp.float32),
            pltpu.SemaphoreType.DMA((start, 2)),
        ]
        held += 2 * start * count * own * width * 4
        args.append(before)
    return pl.pallas_call(
        functools.partial(pairs_body, start, pieces),
        out_shape=jax.ShapeDtypeStruct((planes, 2 * planes, own, width), jnp.float32),
        in_specs=[vmem] * (2 * pieces) + [hbm] * (1 if start else 0),
        out_specs=hbm,
        scratch_shapes=scratch,
        input_output_aliases={2 * pieces: 0} if start else {},
        compiler_params=pltpu.CompilerParams(vmem_limit_bytes=held + (6 << 20)),
        cost_estimate=pl.CostEstimate(
            flops=6 * held // 4, bytes_accessed=held, transcendentals=0
        ),
    )(*args)


def partner(groups, bits):
    return [(i, i ^ bits) for i in range(groups)]


def sent(send, groups, bits):
    return lax.ppermute(send, "band", partner(groups, bits))


def halve(keep, send, groups, bit):
    got = sent(send, groups, bit)
    halves = (-1, 2, *keep.shape[1:])
    keep, got = keep.reshape(halves), got.reshape(halves)
    send = (keep[:, 1] + got[:, 1].astype(jnp.float32)).astype(jnp.bfloat16)
    keep, got, send = lax.optimization_barrier((keep, got, send))
    keep = lax.optimization_barrier(keep[:, 0] + got[:, 0].astype(jnp.float32))
    return keep, send


def two_paths(keeps, sends, count, groups):
    rest = count - keeps.shape[2]
    first = halve(keeps[0], sends[0], groups, 1)
    second = halve(keeps[1, :, :rest], sends[1, :, :rest], groups, 2)
    first = halve(*first, groups, 2)
    second = halve(*second, groups, 1)
    keep, send = (jnp.concatenate(both, axis=1) for both in zip(first, second))
    bit = 4
    while 2 * bit < groups:
        keep, send = halve(keep, send, groups, bit)
        bit *= 2
    got = sent(send, groups, bit)
    return (keep[0] + got[0].astype(jnp.float32)).astype(jnp.bfloat16)


def direct(keep, send, groups):
    got = sent(send, groups, 1)
    order = sorted(range(1, groups // 2), reverse=True)
    sends = [(keep[d] + got[d].astype(jnp.float32)).astype(jnp.bfloat16) for d in order]
    keep, got, *sends = lax.optimization_barrier((keep, got, *sends))
    total = lax.optimization_barrier(keep[0] + got[0].astype(jnp.float32))
    for d, part in zip(order, sends):
        total = total + sent(part, groups, 2 * d).astype(jnp.float32)
    return total.astype(jnp.bfloat16)


def shards(velocity, wave_x, wave_z):
    planes, _, _ = velocity.shape
    groups = lax.axis_size("band")
    modes_x, modes_z = wave_x.shape[0], wave_z.shape[0]
    total = sum(CHUNKS)
    ends = [0]
    for c in CHUNKS:
        ends.append(ends[-1] + c)
    ends = [planes * e // total for e in ends]
    tables = [wave_x[None], wave_z[None]]
    mine, others, out = [], [], None
    for chunk, (start, stop) in enumerate(zip(ends[:-1], ends[1:])):
        got = transform(
            velocity, tables, start, stop - start, BLOCKS[chunk], BLOCKS[-1], 1 + chunk, groups, modes_x, modes_z
        )
        tables = [*got[2:4], *got[4:]] if start == 0 else [*tables[:2], *got[2:]]
        keep, send = got[:2]
        if chunk == 0:
            piece = direct(keep[0], send[0], groups)
        else:
            piece = two_paths(keep, send, stop - start, groups)
        mine.append(piece)
        others.append(lax.ppermute(piece, "plane", [(0, 1), (1, 0)]))
        out = pairs(mine, others, start, planes, out)
    return out.transpose(2, 0, 1, 3)


def solution(mesh):
    in_specs = (P(("snap", "plane"), "band", None), P(), P())
    out_specs = P("band", ("snap", "plane"), None, None)
    return jax.shard_map(shards, mesh=mesh, in_specs=in_specs, out_specs=out_specs, check_vma=False)
```

```python
import functools
import math

import jax
import jax.numpy as jnp
from jax import lax
from jax.experimental import pallas as pl
from jax.experimental.pallas import tpu as pltpu
from jax.sharding import PartitionSpec as P


full_turn = 2.0 * math.pi
CHUNKS = (10, 8)
BLOCKS = (2, 1)
AHEAD = 3


def split(points):
    fine = 1 << (points.bit_length() // 2)
    return fine, points // fine


def cos_sin(phase, points):
    radians = (phase & (points - 1)).astype(jnp.float32) * (full_turn / points)
    return jnp.cos(radians), jnp.sin(radians)


def fill_table(wave, offset, amount, points, store):
    fine, coarse = split(amount)
    lanes = wave.shape[1]
    row = lax.broadcasted_iota(jnp.int32, (fine, lanes), 0)
    cos_b, sin_b = cos_sin(row * wave, points)
    factor = 1.0 / math.sqrt(points)
    cos_b, sin_b = cos_b * factor, sin_b * factor
    batch = 8
    row = lax.broadcasted_iota(jnp.int32, (batch, lanes), 0)

    def fill(g, carry):
        cos_a, sin_a = cos_sin((offset + (row + g * batch) * fine) * wave, points)
        for r in range(batch):
            cos_r, sin_r = cos_a[r : r + 1], sin_a[r : r + 1]
            cosine = (cos_r * cos_b - sin_r * sin_b).astype(jnp.bfloat16)
            sine = (sin_r * cos_b + cos_r * sin_b).astype(jnp.bfloat16)
            store(pl.multiple_of((g * batch + r) * fine, fine), fine, cosine, sine)
        return carry

    lax.fori_loop(0, coarse // batch, fill, 0)


def fill_tables(me, groups, wave_x, wave_z, bx_ref, bz_ref):
    points_x, modes = bx_ref.shape[0], bx_ref.shape[1] // 2
    rows = bz_ref.shape[0] // 2
    own = modes // groups
    wave = jnp.broadcast_to(wave_x, (8, modes))
    lane = lax.broadcasted_iota(jnp.int32, wave.shape, 1)
    bit = 1
    while bit < groups:
        shift = bit * own
        swapped = jnp.where(
            (lane & shift) != 0, pltpu.roll(wave, shift, 1), pltpu.roll(wave, modes - shift, 1)
        )
        wave = jnp.where((me & bit) != 0, swapped, wave)
        bit *= 2

    def store_x(at, size, cosine, sine):
        bx_ref[pl.ds(at, size), :modes] = cosine
        bx_ref[pl.ds(at, size), modes:] = -sine

    def store_z(at, size, cosine, sine):
        bz_ref[pl.ds(at, size), :modes] = cosine
        bz_ref[pl.ds(at, size), modes:] = -sine
        bz_ref[pl.ds(rows + at, size), :modes] = sine
        bz_ref[pl.ds(rows + at, size), modes:] = cosine

    fill_table(wave[:1], 0, points_x, points_x, store_x)
    fill_table(wave_z, me * rows, rows, rows * groups, store_z)


def transform_body(start, count, first, last, groups, vel_ref, *rest):
    if first:
        wave_x_ref, wave_z_ref, *rest = rest
    else:
        bx_ref, bz_ref, _, *rest = rest
    keep_ref, send_ref, *rest = rest
    if first:
        bx_ref, bz_ref, *rest = rest
    if not last:
        next_ref, *rest = rest
    buf, spec, sem, *rest = rest
    paths, half, path_count, own, width = keep_ref.shape
    modes_x = bx_ref.shape[1] // 2
    block = spec.shape[1] // vel_ref.shape[1]
    held = 0 if first else AHEAD

    def fetch(p):
        return pltpu.make_async_copy(vel_ref.at[start + p], buf.at[p], sem.at[p])

    if first:
        waves, wave_sem = rest
        wave_copies = [
            pltpu.make_async_copy(ref, waves.at[i], wave_sem.at[i])
            for i, ref in enumerate((wave_x_ref, wave_z_ref))
        ]
        for copy in wave_copies:
            copy.start()
    early = 1 if first else count
    for p in range(held, early):
        fetch(p).start()
    if first:
        for copy in wave_copies:
            copy.wait()
        for p in range(early, count):
            fetch(p).start()
    if not last:
        ahead = pltpu.make_async_copy(
            vel_ref.at[pl.ds(start + count, AHEAD)], next_ref.at[pl.ds(0, AHEAD)], sem.at[count]
        )
        ahead.start()
    if first:
        fill_tables(lax.axis_index("band"), groups, waves[0], waves[1], bx_ref, bz_ref)

    rows, points = vel_ref.shape[1:]

    def along_x(g, planes):
        out = jnp.dot(
            planes.reshape(block * rows, points), bx_ref[...], preferred_element_type=jnp.float32
        )
        spec[g % 2] = out.astype(jnp.bfloat16)

    def along_z(g, many):
        for k in range(block):
            one = many[k * rows : (k + 1) * rows]
            both = jnp.concatenate([one[:, :modes_x], one[:, modes_x:]], axis=0)
            modes = lax.dot_general(
                both, bz_ref[...], (((0,), (0,)), ((), ())), preferred_element_type=jnp.float32
            ).reshape(half // 2, 2, 2, own, width)
            p = g * block + k
            path = 0
            below, above = modes[:, 1, 0], modes[:, 0, 1]
            if paths == 2:
                path = jnp.asarray(p >= path_count).astype(jnp.int32)
                below, above = jnp.where(path == 1, above, below), jnp.where(path == 1, below, above)
            p = p - path * path_count
            for part in range(half // 2):
                keep_ref[path, 2 * part, p] = modes[part, 0, 0]
                keep_ref[path, 2 * part + 1, p] = below[part]
                send_ref[path, 2 * part, p] = above[part].astype(jnp.bfloat16)
                send_ref[path, 2 * part + 1, p] = modes[part, 1, 1].astype(jnp.bfloat16)

    def arrive(g):
        for k in range(block):
            fetch(g * block + k).wait()

    if first:
        arrive(0)
    along_x(0, buf[:block])

    def step(g, carry):
        if first:
            arrive(g)
        else:
            pl.when(g * block >= held)(lambda: arrive(g))
        before = spec[(g - 1) % 2]
        along_x(g, buf[pl.ds(g * block, block)])
        along_z(g - 1, before)
        return carry

    steps = count // block
    lax.fori_loop(1, steps, step, 0)
    along_z(steps - 1, spec[(steps - 1) % 2])
    if not last:
        ahead.wait()


def transform(velocity, tables, start, count, block, paths, groups, modes_x, modes_z):
    planes, rows, points = velocity.shape
    first, last = start == 0, start + count == planes
    own, half = modes_x // groups, groups // 2
    width = 2 * modes_z
    vmem = pl.BlockSpec(memory_space=pltpu.VMEM)
    hbm = pl.BlockSpec(memory_space=pltpu.HBM)
    outs = [
        jax.ShapeDtypeStruct((paths, half, -(-count // paths), own, width), jnp.float32),
        jax.ShapeDtypeStruct((paths, half, -(-count // paths), own, width), jnp.bfloat16),
    ]
    more = []
    if first:
        outs += [
            jax.ShapeDtypeStruct((points, 2 * modes_x), jnp.bfloat16),
            jax.ShapeDtypeStruct((2 * rows, width), jnp.bfloat16),
        ]
        more = [pltpu.VMEM((2, *tables[0].shape), jnp.int32), pltpu.SemaphoreType.DMA((2,))]
        tables = [pltpu.with_memory_space_constraint(t, pltpu.HBM) for t in tables]
    if not last:
        outs.append(jax.ShapeDtypeStruct((planes - start - count, rows, points), velocity.dtype))
    if not first:
        outs.append(jax.ShapeDtypeStruct((count, rows, points), velocity.dtype))
    scratch = 2 * count * rows * points
    return pl.pallas_call(
        functools.partial(transform_body, start, count, first, last, groups),
        out_shape=outs,
        in_specs=[hbm] + [hbm if first else vmem] * len(tables),
        out_specs=[vmem] * len(outs),
        input_output_aliases={} if first else {3: 2},
        scratch_shapes=[
            *([pltpu.VMEM((count, rows, points), velocity.dtype)] if first else []),
            pltpu.VMEM((2, block * rows, 2 * modes_x), jnp.bfloat16),
            pltpu.SemaphoreType.DMA((count + 1,)),
            *more,
        ],
        compiler_params=pltpu.CompilerParams(vmem_limit_bytes=scratch + (8 << 20)),
        cost_estimate=pl.CostEstimate(
            flops=4 * count * rows * points * modes_x,
            bytes_accessed=scratch,
            transcendentals=0,
        ),
    )(velocity, *tables)


def pairs_body(start, pieces, *refs):
    me = lax.axis_index("plane")
    mine, others = refs[:pieces], refs[pieces : 2 * pieces]
    refs = refs[2 * pieces + (1 if start else 0) :]
    out_ref, both, rows_buf, rows_sem = refs[:4]
    _, stop, _, width = both.shape
    half = width // 2
    planes = out_ref.shape[0]
    for side, group in enumerate((mine, others)):
        at = 0
        for ref in group:
            both[side, at : at + ref.shape[0]] = ref[...].astype(jnp.float32)
            at += ref.shape[0]

    def sweep(first_i, last_i, first_j, buf, sem):
        count = stop - first_j

        def copy(i, g):
            offset = planes * (me if g == 0 else 1 - me)
            return pltpu.make_async_copy(
                buf.at[i - first_i, g],
                out_ref.at[i, pl.ds(offset + first_j, count)],
                sem.at[i - first_i, g],
            )

        def one(i, carry):
            here = both[0, i]
            real_i, imag_i = here[:, :half], here[:, half:]
            for g in range(2):
                for j in range(count):
                    there = both[g, first_j + j]
                    real_j, imag_j = there[:, :half], there[:, half:]
                    buf[i - first_i, g, j, :, :half] = real_i * real_j + imag_i * imag_j
                    buf[i - first_i, g, j, :, half:] = imag_i * real_j - real_i * imag_j
                copy(i, g).start()
            return carry

        lax.fori_loop(first_i, last_i, one, 0)

        def finish():
            def one_wait(i, carry):
                copy(i, 0).wait()
                copy(i, 1).wait()
                return carry

            lax.fori_loop(first_i, last_i, one_wait, 0)

        return finish

    finish = [sweep(start, stop, 0, rows_buf, rows_sem)]
    if start:
        finish.append(sweep(0, start, start, *refs[4:]))
    for wait in finish:
        wait()


def pairs(mine, others, start, planes, before):
    pieces = len(mine)
    _, own, width = mine[0].shape
    count = mine[-1].shape[0]
    stop = start + count
    vmem = pl.BlockSpec(memory_space=pltpu.VMEM)
    hbm = pl.BlockSpec(memory_space=pltpu.HBM)
    scratch = [
        pltpu.VMEM((2, stop, own, width), jnp.float32),
        pltpu.VMEM((count, 2, stop, own, width), jnp.float32),
        pltpu.SemaphoreType.DMA((count, 2)),
    ]
    held = (2 * stop + 2 * count * stop) * own * width * 4
    args = [*mine, *others]
    if start:
        scratch += [
            pltpu.VMEM((start, 2, count, own, width), jnp.float32),
            pltpu.SemaphoreType.DMA((start, 2)),
        ]
        held += 2 * start * count * own * width * 4
        args.append(before)
    return pl.pallas_call(
        functools.partial(pairs_body, start, pieces),
        out_shape=jax.ShapeDtypeStruct((planes, 2 * planes, own, width), jnp.float32),
        in_specs=[vmem] * (2 * pieces) + [hbm] * (1 if start else 0),
        out_specs=hbm,
        scratch_shapes=scratch,
        input_output_aliases={2 * pieces: 0} if start else {},
        compiler_params=pltpu.CompilerParams(vmem_limit_bytes=held + (6 << 20)),
        cost_estimate=pl.CostEstimate(
            flops=6 * held // 4, bytes_accessed=held, transcendentals=0
        ),
    )(*args)


def partner(groups, bits):
    return [(i, i ^ bits) for i in range(groups)]


def sent(send, groups, bits):
    return lax.ppermute(send, "band", partner(groups, bits))


def halve(keep, send, groups, bit):
    got = sent(send, groups, bit)
    halves = (-1, 2, *keep.shape[1:])
    keep, got = keep.reshape(halves), got.reshape(halves)
    send = (keep[:, 1] + got[:, 1].astype(jnp.float32)).astype(jnp.bfloat16)
    keep, got, send = lax.optimization_barrier((keep, got, send))
    keep = lax.optimization_barrier(keep[:, 0] + got[:, 0].astype(jnp.float32))
    return keep, send


def two_paths(keeps, sends, count, groups):
    rest = count - keeps.shape[2]
    first = halve(keeps[0], sends[0], groups, 1)
    second = halve(keeps[1, :, :rest], sends[1, :, :rest], groups, 2)
    first = halve(*first, groups, 2)
    second = halve(*second, groups, 1)
    keep, send = (jnp.concatenate(both, axis=1) for both in zip(first, second))
    bit = 4
    while 2 * bit < groups:
        keep, send = halve(keep, send, groups, bit)
        bit *= 2
    got = sent(send, groups, bit)
    return (keep[0] + got[0].astype(jnp.float32)).astype(jnp.bfloat16)


def direct(keep, send, groups):
    got = sent(send, groups, 1)
    order = sorted(range(1, groups // 2), reverse=True)
    sends = [(keep[d] + got[d].astype(jnp.float32)).astype(jnp.bfloat16) for d in order]
    keep, got, *sends = lax.optimization_barrier((keep, got, *sends))
    total = lax.optimization_barrier(keep[0] + got[0].astype(jnp.float32))
    for d, part in zip(order, sends):
        total = total + sent(part, groups, 2 * d).astype(jnp.float32)
    return total.astype(jnp.bfloat16)


def shards(velocity, wave_x, wave_z):
    planes, _, _ = velocity.shape
    groups = lax.axis_size("band")
    modes_x, modes_z = wave_x.shape[0], wave_z.shape[0]
    total = sum(CHUNKS)
    ends = [0]
    for c in CHUNKS:
        ends.append(ends[-1] + c)
    ends = [planes * e // total for e in ends]
    tables = [wave_x[None], wave_z[None]]
    mine, others, out = [], [], None
    for chunk, (start, stop) in enumerate(zip(ends[:-1], ends[1:])):
        got = transform(
            velocity, tables, start, stop - start, BLOCKS[chunk], 1 + chunk, groups, modes_x, modes_z
        )
        tables = [*got[2:4], *got[4:]] if start == 0 else [*tables[:2], *got[2:]]
        keep, send = got[:2]
        if chunk == 0:
            piece = direct(keep[0], send[0], groups)
        else:
            piece = two_paths(keep, send, stop - start, groups)
        mine.append(piece)
        others.append(lax.ppermute(piece, "plane", [(0, 1), (1, 0)]))
        out = pairs(mine, others, start, planes, out)
    return out.transpose(2, 0, 1, 3)


def solution(mesh):
    in_specs = (P(("snap", "plane"), "band", None), P(), P())
    out_specs = P("band", ("snap", "plane"), None, None)
    return jax.shard_map(shards, mesh=mesh, in_specs=in_specs, out_specs=out_specs, check_vma=False)
```
